32 devices in a mesh: seq: 16 (over z, y, x), head: 2 (over core).
Axes of the slice: x: 2, y: 2, z: 4, core: 2. Of those that a mesh axis runs over, the one named last changes fastest.
Arguments:
- queries: bfloat16 [4096, 2048], P('seq', 'head'), may hold values from -6 to 6
- key_rows: bfloat16 [4096, 2048], P('seq', 'head'), may hold values from -6 to 6
- value_rows: bfloat16 [4096, 2048], P('seq', 'head'), may hold values from -6 to 6
- out_weight: bfloat16 [2048, 2048], P('head'), may hold values from -3 to 3
Outputs:
- layer_out: bfloat16 [4096, 2048], P('seq', 'head')
The draws below stay inside these ranges and needn't reach their ends.
All inputs are finite; a program needn't handle non-finite values.
Results may differ from the reference program's by a relative error of at most 0.012.
Values may be sent and summed in bfloat16 or wider, within the bound.
A program may use at most 64 MiB of HBM per device.

```python
import jax
import jax.numpy as jnp
from jax import lax

HEADS = 16
HEAD_DIM = 128
LEAF = 256
LEVELS = 3
D = 2048
TOKENS = 4096
N_HEAD = 2


def run_mixed(key, salt):
    shared_draw = jax.random.normal(jax.random.fold_in(key, salt), (TOKENS // 8, D), jnp.float32)
    shared_rows = jnp.repeat(shared_draw, 8, axis=0)
    noise_rows = jax.random.normal(jax.random.fold_in(key, salt + 100), (TOKENS, D), jnp.float32)
    return jnp.clip(0.8 * shared_rows + 0.6 * noise_rows, -6.0, 6.0)


def draw_queries(key, part):
    base_draw = run_mixed(key, 11)
    return base_draw.astype(jnp.bfloat16)


def draw_key_rows(key, part):
    base_draw = run_mixed(key, 12)
    return base_draw.astype(jnp.bfloat16)


def steps_of(rng, extent, shards, smallest, top_value):
    def one(dim, parts):
        heights = jax.random.uniform(jax.random.fold_in(jax.random.fold_in(rng, 6), dim), (parts,), jnp.float32, smallest / len(shards), top_value / len(shards))
        return jnp.repeat(jnp.exp(heights), extent[dim] // parts).reshape((-1,) + (1,) * (len(extent) - dim - 1))

    level = one(*shards[0])
    for cut in shards[1:]:
        level = level * one(*cut)
    return level


def gaussian(own_key, extent, scale, limit, split=(), held_as=jnp.bfloat16):
    level = steps_of(own_key, extent, split, -0.22, 0.18) if split else 1.0
    array = jax.random.normal(own_key, extent, jnp.float32) * scale * level
    return jnp.minimum(jnp.maximum(array, -limit), limit).astype(held_as)


def setup_inputs(seed: int = 0) -> dict:
    keys = jax.random.split(jax.random.key(seed), 5)
    queries = draw_queries(jax.random.fold_in(keys[4], 71), 0)
    key_rows = draw_key_rows(jax.random.fold_in(keys[4], 71), 0)
    value_rows = gaussian(keys[2], (TOKENS, D), 1.0, 6.0, ((0, 16), (1, 2)))
    out_weight = gaussian(keys[3], (D, D), 0.5, 3.0, ((0, 2),))
    return dict(queries=queries, key_rows=key_rows, value_rows=value_rows, out_weight=out_weight)


def averaged(matrix, factor):
    blocks = matrix.shape[0] // factor
    folded = matrix.astype(jnp.float32).reshape(blocks, factor, matrix.shape[1])
    return jnp.mean(folded, axis=1).astype(jnp.bfloat16)


def level_attention(level_q, level_k, level_v, centred):
    blocks = level_q.shape[0] // LEAF
    padding = jnp.zeros((LEAF, level_k.shape[1]), level_k.dtype)
    padded_keys = jnp.concatenate([padding, level_k, padding], 0).reshape(blocks + 2, LEAF, HEADS, HEAD_DIM)
    padded_values = jnp.concatenate([padding, level_v, padding], 0).reshape(blocks + 2, LEAF, HEADS, HEAD_DIM)
    query_blocks = level_q.reshape(blocks, LEAF, HEADS, HEAD_DIM)
    scaling = HEAD_DIM ** -0.5

    def one_block(inputs):
        block_index, query_tile = inputs
        window_keys = lax.dynamic_slice_in_dim(padded_keys, block_index, 3, 0)
        window_values = lax.dynamic_slice_in_dim(padded_values, block_index, 3, 0)
        lower_ok = block_index > 0
        upper_ok = block_index < blocks - 1
        if centred:
            segments = jnp.stack([lower_ok, jnp.asarray(True), upper_ok])
        else:
            window_keys = jnp.concatenate([window_keys[0:1], window_keys[2:3]], 0)
            window_values = jnp.concatenate([window_values[0:1], window_values[2:3]], 0)
            segments = jnp.stack([lower_ok, upper_ok])
        usable = jnp.repeat(segments, LEAF)
        keys_flat = window_keys.reshape(-1, HEADS, HEAD_DIM).astype(jnp.float32)
        values_flat = window_values.reshape(-1, HEADS, HEAD_DIM).astype(jnp.float32)
        scores = jnp.einsum("qhd,khd->hqk", query_tile.astype(jnp.float32), keys_flat) * scaling
        scores = jnp.where(usable[None, None, :], scores, -jnp.inf)
        maxima = jnp.max(scores, axis=-1)
        weights = jnp.exp(scores - maxima[..., None]).astype(jnp.bfloat16)
        totals = jnp.sum(weights.astype(jnp.float32), axis=-1)
        numerator = jnp.einsum("hqk,khd->qhd", weights.astype(jnp.float32), values_flat)
        return maxima.T, totals.T, numerator

    maxima, totals, numerator = lax.map(one_block, (jnp.arange(blocks, dtype=jnp.int32), query_blocks))
    row_count = blocks * LEAF
    return maxima.reshape(row_count, HEADS), totals.reshape(row_count, HEADS), numerator.reshape(row_count, HEADS, HEAD_DIM)


def reference(queries, key_rows, value_rows, out_weight):
    row_count = queries.shape[0]
    results = []
    for level_index in range(LEVELS + 1):
        factor = 2 ** level_index
        if level_index == 0:
            level_q, level_k, level_v = queries, key_rows, value_rows
        else:
            level_q = averaged(queries, factor)
            level_k = averaged(key_rows, factor)
            level_v = averaged(value_rows, factor)
        maxima, totals, numerator = level_attention(level_q, level_k, level_v, level_index == 0)
        results.append((factor, maxima, totals, numerator))
    row_max = results[0][1]
    for entry in results[1:]:
        factor, maxima = entry[0], entry[1]
        spread = jnp.broadcast_to(maxima[:, None, :], (maxima.shape[0], factor, HEADS)).reshape(row_count, HEADS)
        row_max = jnp.maximum(row_max, spread)
    denominator = jnp.zeros((row_count, HEADS), jnp.float32)
    numer_all = jnp.zeros((row_count, HEADS, HEAD_DIM), jnp.float32)
    for entry in results:
        factor, maxima, totals, numerator = entry
        blocks = maxima.shape[0]
        local_max = row_max.reshape(blocks, factor, HEADS)
        weight_level = factor * jnp.exp(maxima[:, None, :] - local_max)
        denominator = denominator + (weight_level * totals[:, None, :]).reshape(row_count, HEADS)
        numer_all = numer_all + (weight_level[..., None] * numerator[:, None, :, :]).reshape(row_count, HEADS, HEAD_DIM)
    attended = (numer_all / denominator[..., None]).reshape(row_count, HEADS * HEAD_DIM).astype(jnp.bfloat16)
    group_width = HEADS * HEAD_DIM // N_HEAD
    output = jnp.zeros((row_count, HEADS * HEAD_DIM), jnp.float32)
    for group_index in range(N_HEAD):
        first_row = group_index * group_width
        partial_value = jnp.dot(attended[:, first_row:first_row + group_width], out_weight[first_row:first_row + group_width], preferred_element_type=jnp.float32).astype(jnp.bfloat16)
        partial_value = lax.optimization_barrier(partial_value)
        output = output + partial_value.astype(jnp.float32)
    return output.astype(jnp.bfloat16)
```

```python
import functools
import math

import jax
import jax.numpy as jnp
from jax import lax
from jax.experimental import pallas as pl
from jax.experimental.pallas import tpu as pltpu
from jax.sharding import PartitionSpec as P

HEAD_DIM = 128
LEAF = 256
LEVELS = 3
GROUP = 2 ** (LEVELS - 1)
MESH = pl.DeviceIdType.MESH
SCALE = HEAD_DIM ** (-0.5) * math.log2(math.e)
LOWEST = -1e30
F32 = jnp.float32
BF16 = jnp.bfloat16


def dot(a, b):
    return lax.dot_general(a, b, (((1,), (0,)), ((), ())), preferred_element_type=F32)


def dot_t(a, b):
    return lax.dot_general(a, b, (((1,), (1,)), ((), ())), preferred_element_type=F32)


def mean_matrix(rows):
    parts = []
    for level in range(1, LEVELS + 1):
        factor = 2**level
        r = lax.broadcasted_iota(jnp.int32, (rows // factor, rows), 0)
        c = lax.broadcasted_iota(jnp.int32, (rows // factor, rows), 1)
        parts.append(jnp.where(c // factor == r, 1.0 / factor, 0.0).astype(BF16))
    return parts


def order_of(i, rows):
    row = (i % (rows // 2**LEVELS)) * 2**LEVELS
    for bit in range(LEVELS):
        row = row + ((i // (rows // 2 ** (bit + 1))) % 2) * 2**bit
    return row


def attend(q, k, v, bias, before):
    s = dot_t(q, k)
    if bias is not None:
        s = s + bias
    top = jnp.max(s, axis=1, keepdims=True) * SCALE
    if before is not None:
        coarse_top, coarse_num = before
        top = jnp.maximum(top, coarse_top[:, :1])
    w = jnp.exp2(s * SCALE - top).astype(BF16)
    num = dot(w, jnp.concatenate([v, jnp.ones((v.shape[0], HEAD_DIM), BF16)], 1))
    if before is not None:
        a = 2.0 * jnp.exp2(coarse_top - top)
        num = num + jnp.concatenate([a, a], 1) * coarse_num
    return top, num


def twice(x, pieces):
    n = x.shape[0] // pieces
    out = []
    for i in range(pieces):
        out += [x[i * n : (i + 1) * n], x[i * n : (i + 1) * n]]
    return jnp.concatenate(out, 0)


def kernel(
    S, NH, q_ref, k_ref, v_ref, w_ref, o_ref,
    kv0, kv1, kv2, kv2own, kv3, c3, qp, q0, q1, q2, q3, n1, m1,
    attbuf, arecv, att, wv, psend, precv,
    s_kv, r_kv, s_q, r_q, s_l3, r_l3, s_z, r_z, s_a, r_a, s_p, r_p, s_w,
):
    rows, width = q_ref.shape
    G = GROUP
    w = width // G
    hg = w // HEAD_DIM
    NG = S // G
    s = lax.axis_index("seq")
    h = lax.axis_index("head")
    g = s // G
    p = s % G
    c = g // 2
    blocks3 = NG // 2
    has_lo, has_hi = g > 0, g < NG - 1
    has_lo3, has_hi3 = c > 0, c < blocks3 - 1
    r1, r2, r3 = rows // 2, rows // 4, rows // 8

    copy_w = pltpu.make_async_copy(w_ref, wv, s_w)
    copy_w.start()

    def cols(i):
        return pl.ds(pl.multiple_of(i * w, HEAD_DIM), w)

    def remote(src, dst, ss, rs, seq, head=None):
        ids = {"seq": seq} if head is None else {"head": head}
        return pltpu.make_async_remote_copy(
            src_ref=src, dst_ref=dst, send_sem=ss, recv_sem=rs, device_id=ids, device_id_type=MESH
        )

    barrier = pltpu.get_barrier_semaphore()
    for i in range(1, G):
        pl.semaphore_signal(barrier, 1, device_id={"seq": g * G + (p + i) % G}, device_id_type=MESH)
    for i in range(1, NH):
        pl.semaphore_signal(barrier, 1, device_id={"head": (h + i) % NH}, device_id_type=MESH)
    sibling = g + 1 - 2 * (g % 2)
    pl.semaphore_signal(barrier, 1, device_id={"seq": sibling * G + p}, device_id_type=MESH)
    for has, dc in ((has_lo3, -1), (has_hi3, 1)):
        @pl.when(has)
        def _():
            for u in range(2):
                for j in range(G):
                    pl.semaphore_signal(
                        barrier, 1, device_id={"seq": (2 * (c + dc) + u) * G + j}, device_id_type=MESH
                    )
    m1_, m2_, m3_ = mean_matrix(rows)
    c3[0] = dot(m3_, k_ref[...]).astype(BF16)
    c3[1] = dot(m3_, v_ref[...]).astype(BF16)
    sides = jnp.where(has_lo3, 1, 0) + jnp.where(has_hi3, 1, 0)
    pl.semaphore_wait(barrier, G - 1 + NH - 1 + 1 + 2 * G * sides)

    def l3_send(side, u, j):
        dc = (-1, 1)[side]
        slot = (2, 0)[side] + g % 2
        return remote(
            c3.at[:, :, cols(j)], kv3.at[:, slot, pl.ds(pl.multiple_of(p * r3, r3), r3)],
            s_l3.at[side, u, j], r_l3.at[slot, p], (2 * (c + dc) + u) * G + j,
        )

    def l3_recv(side, u, j):
        slot = 2 * side + u
        dc = (-1, 1)[side]
        return remote(
            c3.at[:, :, cols(j)], kv3.at[:, slot, pl.ds(j * r3, r3)],
            s_l3.at[side, u, j], r_l3.at[slot, j], (2 * (c + dc) + u) * G + j,
        )

    sides3 = ((0, has_lo3), (1, has_hi3))
    for side, has in sides3:
        @pl.when(has)
        def _():
            for j in range(G):
                for u in range(2):
                    l3_send(side, u, j).start()

    kv_refs = (k_ref, v_ref)

    def kv_send(i, t):
        d = (p + i) % G
        return remote(kv_refs[t].at[:, cols(d)], kv0.at[t, 1 + p], s_kv.at[t, i], r_kv.at[t, i], g * G + d)

    def kv_recv(i, t):
        d = (p + G - i) % G
        return remote(kv_refs[t].at[:, cols(d)], kv0.at[t, 1 + d], s_kv.at[t, i], r_kv.at[t, i], g * G + d)

    order = (2, 1, 3) if G == 4 else tuple(range(1, G))
    order = tuple(sorted(range(1, G), key=lambda i: order.index(i) if i in order else i))
    for t in range(2):
        for i in order:
            kv_send(i, t).start()

    i_ = lax.broadcasted_iota(jnp.int32, (rows, rows), 0)
    t_ = lax.broadcasted_iota(jnp.int32, (rows, rows), 1)
    perm = jnp.where(order_of(i_, rows) == t_, 1.0, 0.0).astype(BF16)
    qp[...] = dot(perm, q_ref[...]).astype(BF16)

    def q_send(i):
        d = (p + i) % G
        return remote(qp.at[:, cols(d)], q0.at[p], s_q.at[i], r_q.at[i], g * G + d)

    def q_recv(i):
        d = (p + G - i) % G
        return remote(qp.at[:, cols(d)], q0.at[d], s_q.at[i], r_q.at[i], g * G + d)

    for i in order:
        q_send(i).start()

    kv0[0, 1 + p] = k_ref[:, cols(p)]
    kv0[1, 1 + p] = v_ref[:, cols(p)]
    q0[p] = qp[:, cols(p)]

    for has, b0, b1, b2 in ((has_lo, 0, 0, 0), (has_hi, G + 1, 3, 1)):
        @pl.when(jnp.logical_not(has))
        def _():
            kv0[:, b0] = jnp.zeros((2, rows, w), BF16)
            kv1[:, b1] = jnp.zeros((2, LEAF, w), BF16)
            kv2[:, b2] = jnp.zeros((2, LEAF, w), BF16)
    for side, has in sides3:
        @pl.when(jnp.logical_not(has))
        def _():
            kv3[:, 2 * side : 2 * side + 2] = jnp.zeros((2, 2, LEAF // 2, w), BF16)

    for t in range(2):
        for i in order:
            kv_recv(i, t).wait_recv()

    def z_pair(dirn, kind):
        last = dirn == 0
        if kind == 0:
            src, dst = (kv0.at[:, G], kv0.at[:, 0]) if last else (kv0.at[:, 1], kv0.at[:, G + 1])
        elif kind == 1:
            a, b = (0, LEAF - r2) if last else (r2, LEAF - r2)
            src, dst = kv2own.at[:, pl.ds(a, b)], kv2.at[:, 0 if last else 1, pl.ds(a, b)]
        else:
            a, b = (0, LEAF - r1) if last else (r1, LEAF - r1)
            src = kv1.at[:, 2 if last else 1, pl.ds(a, b)]
            dst = kv1.at[:, 0 if last else 3, pl.ds(a, b)]
        to = s + G if last else s - G
        return remote(src, dst, s_z.at[dirn, kind], r_z.at[dirn, kind], to)

    dirs = ((0, has_hi), (1, has_lo))
    comes = ((0, has_lo), (1, has_hi))

    def z_start(kind):
        for dirn, has in dirs:
            @pl.when(has)
            def _():
                z_pair(dirn, kind).start()

    def z_wait(kind):
        for dirn, has in comes:
            @pl.when(has)
            def _():
                z_pair(dirn, kind).wait_recv()

    z_start(0)
    for j in range(G):
        for t in range(2):
            x = kv0[t, 1 + j]
            kv2own[t, j * r2 : (j + 1) * r2] = dot(m2_, x).astype(BF16)
    z_start(1)
    for j in range(G):
        for t in range(2):
            x = kv0[t, 1 + j]
            kv1[t, 1 + j // 2, (j % 2) * r1 : (j % 2 + 1) * r1] = dot(m1_, x).astype(BF16)
    z_start(2)

    for i in order:
        q_recv(i).wait_recv()
    for j in range(G):
        x = q0[j].astype(F32)
        x = x[:r1] + x[r1:]
        q1[j] = (x * 0.5).astype(BF16)
        x = x[:r2] + x[r2:]
        q2[j] = (x * 0.25).astype(BF16)
        x = x[:r3] + x[r3:]
        q3[j] = (x * 0.125).astype(BF16)

    def bias_of(keys, lo, hi):
        col = lax.broadcasted_iota(jnp.int32, (1, keys), 1)
        b_lo = jnp.where(lo, 0.0, LOWEST)
        b_hi = jnp.where(hi, 0.0, LOWEST)
        return jnp.where(col < LEAF, b_lo, jnp.where(col >= keys - LEAF, b_hi, 0.0))

    def wide(x):
        return jnp.broadcast_to(x, (x.shape[0], HEAD_DIM))

    for side, has in sides3:
        @pl.when(has)
        def _():
            for u in range(2):
                for j in range(G):
                    l3_recv(side, u, j).wait_recv()

    state = []
    for hh in range(hg):
        lanes = slice(hh * HEAD_DIM, (hh + 1) * HEAD_DIM)
        top, num = attend(
            q3[:, :, lanes].reshape(G * r3, HEAD_DIM),
            kv3[0, :, :, lanes].reshape(2 * LEAF, HEAD_DIM),
            kv3[1, :, :, lanes].reshape(2 * LEAF, HEAD_DIM),
            bias_of(2 * LEAF, has_lo3, has_hi3), None,
        )
        state.append((twice(wide(top), G), twice(num, G)))

    z_wait(0)
    for has, b0, b1, a1, b2, a2 in (
        (has_lo, 0, 0, LEAF - r1, 0, LEAF - r2), (has_hi, G + 1, 3, 0, 1, 0)
    ):
        @pl.when(has)
        def _():
            for t in range(2):
                x = kv0[t, b0]
                kv1[t, b1, a1 : a1 + r1] = dot(m1_, x).astype(BF16)
                kv2[t, b2, a2 : a2 + r2] = dot(m2_, x).astype(BF16)
    z_wait(1)
    for hh in range(hg):
        lanes = slice(hh * HEAD_DIM, (hh + 1) * HEAD_DIM)
        top, num = attend(
            q2[:, :, lanes].reshape(G * r2, HEAD_DIM),
            kv2[0, :, :, lanes].reshape(2 * LEAF, HEAD_DIM),
            kv2[1, :, :, lanes].reshape(2 * LEAF, HEAD_DIM),
            bias_of(2 * LEAF, has_lo, has_hi), state[hh],
        )
        state[hh] = (twice(wide(top), G), twice(num, G))
    z_wait(2)
    for hh in range(hg):
        lanes = slice(hh * HEAD_DIM, (hh + 1) * HEAD_DIM)
        for b in range(2):
            part = slice(b * LEAF, (b + 1) * LEAF)
            top, num = attend(
                q1[2 * b : 2 * b + 2, :, lanes].reshape(LEAF, HEAD_DIM),
                jnp.concatenate([kv1[0, b, :, lanes], kv1[0, b + 2, :, lanes]], 0),
                jnp.concatenate([kv1[1, b, :, lanes], kv1[1, b + 2, :, lanes]], 0),
                bias_of(2 * LEAF, has_lo if b == 0 else True, has_hi if b == 1 else True),
                (state[hh][0][part], state[hh][1][part]),
            )
            m1[hh, 2 * b : 2 * b + 2] = wide(top).reshape(2, r1, HEAD_DIM)
            n1[hh, 2 * b : 2 * b + 2] = num.reshape(2, r1, 2 * HEAD_DIM)

    def a_send(i, j):
        return remote(attbuf.at[j], arecv.at[p], s_a.at[i], r_a.at[i], g * G + j)

    def a_recv(i):
        d = (p + G - i) % G
        return remote(attbuf.at[d], arecv.at[d], s_a.at[i], r_a.at[i], g * G + d)

    def level0(step, carry):
        i = (step + 1) % G
        j = (p + i) % G
        bias = bias_of(3 * LEAF, jnp.logical_or(has_lo, j > 0), jnp.logical_or(has_hi, j < G - 1))
        for hh in range(hg):
            lanes = slice(hh * HEAD_DIM, (hh + 1) * HEAD_DIM)
            top, num = attend(
                q0[j, :, lanes],
                kv0[0, pl.ds(j, 3), :, lanes].reshape(3 * LEAF, HEAD_DIM),
                kv0[1, pl.ds(j, 3), :, lanes].reshape(3 * LEAF, HEAD_DIM),
                bias, (twice(m1[hh, j], 1), twice(n1[hh, j], 1)),
            )
            attbuf[j, :, lanes] = (num[:, :HEAD_DIM] / num[:, HEAD_DIM:]).astype(BF16)

        @pl.when(step < G - 1)
        def _():
            a_send(i, j).start()

        return carry

    lax.fori_loop(0, G, level0, 0)

    arecv[p] = attbuf[p]
    for i in range(1, G):
        a_recv(i).wait_recv()
    back = jnp.where(order_of(t_, rows) == i_, 1.0, 0.0).astype(BF16)
    for i in range(G):
        att[:, i * w : (i + 1) * w] = dot(back, arecv[i]).astype(BF16)

    copy_w.wait()
    cw = o_ref.shape[1]
    chunks = psend.shape[1]
    ch = cw // chunks

    def p_copy(i, n, peer):
        return remote(psend.at[i - 1, n], precv.at[i - 1, n], s_p.at[i - 1, n], r_p.at[i - 1, n], None, peer)

    for i in range(1, NH):
        t = (h + i) % NH
        for n in range(chunks):
            at = pl.multiple_of(t * cw + n * ch, HEAD_DIM)
            psend[i - 1, n] = dot(att[...], wv[:, pl.ds(at, ch)]).astype(BF16)
            p_copy(i, n, t).start()
    for n in range(chunks):
        at = pl.multiple_of(h * cw + n * ch, HEAD_DIM)
        total = dot(att[...], wv[:, pl.ds(at, ch)]).astype(BF16).astype(F32)
        for i in range(1, NH):
            p_copy(i, n, (h + NH - i) % NH).wait_recv()
            total = total + precv[i - 1, n].astype(F32)
        o_ref[:, n * ch : (n + 1) * ch] = total.astype(o_ref.dtype)

    for side, has in sides3:
        @pl.when(has)
        def _():
            for j in range(G):
                for u in range(2):
                    l3_send(side, u, j).wait_send()
    for i in order:
        for t in range(2):
            kv_send(i, t).wait_send()
        q_send(i).wait_send()
        a_send(i, (p + i) % G).wait_send()
    for kind in range(3):
        for dirn, has in dirs:
            @pl.when(has)
            def _():
                z_pair(dirn, kind).wait_send()
    for i in range(1, NH):
        for n in range(chunks):
            p_copy(i, n, (h + i) % NH).wait_send()


def solution(mesh):
    S, NH = mesh.shape["seq"], mesh.shape["head"]

    def body(queries, key_rows, value_rows, out_weight):
        rows, width = queries.shape
        full = out_weight.shape[1]
        G = GROUP
        w = width // G
        hg = w // HEAD_DIM
        assert rows == LEAF and S % (2 * G) == 0 and S >= 4 * G and w % HEAD_DIM == 0
        cw = full // NH
        chunks = 2
        vmem = pl.BlockSpec(memory_space=pltpu.VMEM)
        dma = pltpu.SemaphoreType.DMA
        V = pltpu.VMEM
        return pl.pallas_call(
            functools.partial(kernel, S, NH),
            out_shape=jax.ShapeDtypeStruct((rows, cw), queries.dtype),
            in_specs=[vmem, vmem, vmem, pl.BlockSpec(memory_space=pl.ANY)],
            out_specs=vmem,
            scratch_shapes=[
                V((2, G + 2, rows, w), BF16),
                V((2, 4, LEAF, w), BF16),
                V((2, 2, LEAF, w), BF16),
                V((2, LEAF, w), BF16),
                V((2, 4, LEAF // 2, w), BF16),
                V((2, rows // 8, width), BF16),
                V((rows, width), BF16),
                V((G, rows, w), BF16),
                V((G, rows // 2, w), BF16),
                V((G, rows // 4, w), BF16),
                V((G, rows // 8, w), BF16),
                V((hg, G, rows // 2, 2 * HEAD_DIM), F32),
                V((hg, G, rows // 2, HEAD_DIM), F32),
                V((G, rows, w), BF16),
                V((G, rows, w), BF16),
                V((rows, width), BF16),
                V((width, full), BF16),
                V((NH - 1, chunks, rows, cw // chunks), BF16),
                V((NH - 1, chunks, rows, cw // chunks), BF16),
                dma((2, G)), dma((2, G)),
                dma((G,)), dma((G,)),
                dma((2, 2, G)), dma((4, G)),
                dma((2, 3)), dma((2, 3)),
                dma((G,)), dma((G,)),
                dma((NH - 1, chunks)), dma((NH - 1, chunks)),
                dma,
            ],
            compiler_params=pltpu.CompilerParams(
                collective_id=0, has_side_effects=True, vmem_limit_bytes=56 * 2**20
            ),
        )(queries, key_rows, value_rows, out_weight)

    in_specs = (P("seq", "head"), P("seq", "head"), P("seq", "head"), P("head", None))
    return jax.shard_map(body, mesh=mesh, in_specs=in_specs, out_specs=P("seq", "head"), check_vma=False)
```

```python
import functools
import math

import jax
import jax.numpy as jnp
from jax import lax
from jax.experimental import pallas as pl
from jax.experimental.pallas import tpu as pltpu
from jax.sharding import PartitionSpec as P

HEAD_DIM = 128
LEAF = 256
LEVELS = 3
GROUP = 2 ** (LEVELS - 1)
MESH = pl.DeviceIdType.MESH
SCALE = HEAD_DIM ** (-0.5) * math.log2(math.e)
LOWEST = -1e30
F32 = jnp.float32
BF16 = jnp.bfloat16
VMEM_BYTES = 56 * 2**20


def dot(a, b):
    return lax.dot_general(a, b, (((1,), (0,)), ((), ())), preferred_element_type=F32)


def dot_t(a, b):
    return lax.dot_general(a, b, (((1,), (1,)), ((), ())), preferred_element_type=F32)


def iota2(n, m):
    shape = (n, m)
    return lax.broadcasted_iota(jnp.int32, shape, 0), lax.broadcasted_iota(jnp.int32, shape, 1)


def mean_matrix(rows, level):
    r, c = iota2(rows >> level, rows)
    return jnp.where((c >> level) == r, 0.5**level, 0.0).astype(BF16)


def order_of(i, rows):
    top = rows.bit_length() - 1
    row = (i & (rows // 2**LEVELS - 1)) << LEVELS
    for bit in range(LEVELS):
        row = row | (((i >> (top - 1 - bit)) & 1) << bit)
    return row


def flip(p, i, bits):
    out = 0
    for b in range(bits):
        out = out + 2**b * ((p // 2**b + i // 2**b) % 2)
    return out


def attend(q, k, v, bias, before):
    s = dot_t(q, k)
    if bias is not None:
        s = s + bias
    top = jnp.max(s, axis=1, keepdims=True) * SCALE
    if before is not None:
        coarse_top, coarse_num = before
        top = jnp.maximum(top, coarse_top[:, :1])
    w = jnp.exp2(s * SCALE - top).astype(BF16)
    num = dot(w, jnp.concatenate([v, jnp.ones((v.shape[0], HEAD_DIM), BF16)], 1))
    if before is not None:
        a = 2.0 * jnp.exp2(coarse_top - top)
        num = num + jnp.concatenate([a, a], 1) * coarse_num
    return top, num


def twice(x, pieces):
    n = x.shape[0] // pieces
    out = []
    for i in range(pieces):
        out += [x[i * n : (i + 1) * n], x[i * n : (i + 1) * n]]
    return jnp.concatenate(out, 0)


def kernel(
    S, NH, q_hbm, k_hbm, v_hbm, w_hbm, o_ref,
    kv0, kv1, kv2, kv2own, kv3, c3, kvm, qm, qp, q0, q1, q2, q3, n1, m1,
    attbuf, arecv, att, wv, psend, precv,
    s_kv, r_kv, s_q, r_q, s_l3, r_l3, s_z, r_z, s_a, r_a, s_p, r_p, s_w, s_in, s_own,
):
    rows, width = q_hbm.shape
    G = GROUP
    D = HEAD_DIM
    w = width // G
    hg = w // D
    NG = S // G
    bits = G.bit_length() - 1
    s = lax.axis_index("seq")
    h = lax.axis_index("head")
    g = s // G
    p = s % G
    c = g // 2
    blocks3 = NG // 2
    has_lo, has_hi = g > 0, g < NG - 1
    has_lo3, has_hi3 = c > 0, c < blocks3 - 1
    sides3 = ((0, has_lo3), (1, has_hi3))
    r1, r2, r3 = rows // 2, rows // 4, rows // 8
    heads = range(hg)
    others = tuple(range(G - 1, 0, -1))

    barrier = pltpu.get_barrier_semaphore()
    for i in others:
        pl.semaphore_signal(barrier, 1, device_id={"seq": g * G + flip(p, i, bits)}, device_id_type=MESH)
    for i in range(1, NH):
        pl.semaphore_signal(barrier, 1, device_id={"head": (h + i) % NH}, device_id_type=MESH)
    sibling = g + 1 - 2 * (g % 2)
    pl.semaphore_signal(barrier, 1, device_id={"seq": sibling * G + p}, device_id_type=MESH)
    for has, dc in ((has_lo3, -1), (has_hi3, 1)):
        @pl.when(has)
        def _():
            for u in range(2):
                for j in range(G):
                    pl.semaphore_signal(
                        barrier, 1, device_id={"seq": (2 * (c + dc) + u) * G + j}, device_id_type=MESH
                    )

    kv_hbm = (k_hbm, v_hbm)
    loads = [pltpu.make_async_copy(kv_hbm[t], kvm.at[t], s_in.at[t]) for t in range(2)]
    loads.append(pltpu.make_async_copy(q_hbm, qm, s_in.at[2]))
    for load in (loads[2], loads[0], loads[1]):
        load.start()
    copy_w = pltpu.make_async_copy(w_hbm, wv, s_w)

    def lanes_of(i, hh):
        return pl.ds(pl.multiple_of((i * hg + hh) * D, D), D)

    def remote(src, dst, ss, rs, seq, head=None):
        ids = {"seq": seq} if head is None else {"head": head}
        return pltpu.make_async_remote_copy(
            src_ref=src, dst_ref=dst, send_sem=ss, recv_sem=rs, device_id=ids, device_id_type=MESH
        )

    own = []
    for hh in heads:
        for t in range(2):
            own.append(
                pltpu.make_async_copy(kv_hbm[t].at[:, lanes_of(p, hh)], kv0.at[hh, t, 1 + p], s_own.at[hh, t])
            )
            own[-1].start()

    sides = jnp.where(has_lo3, 1, 0) + jnp.where(has_hi3, 1, 0)
    pl.semaphore_wait(barrier, G - 1 + NH - 1 + 1 + 2 * G * sides)

    def kv_send(hh, t, i):
        d = flip(p, i, bits)
        return remote(
            kv_hbm[t].at[:, lanes_of(d, hh)], kv0.at[hh, t, 1 + p], s_kv.at[hh, t, i], r_kv.at[hh, t, i], g * G + d
        )

    def kv_recv(hh, t, i):
        d = flip(p, i, bits)
        return remote(
            kv_hbm[t].at[:, lanes_of(d, hh)], kv0.at[hh, t, 1 + d], s_kv.at[hh, t, i], r_kv.at[hh, t, i], g * G + d
        )

    for hh in heads:
        for t in range(2):
            for i in others:
                kv_send(hh, t, i).start()
    copy_w.start()

    def l3_send(side, u, j):
        dc = (-1, 1)[side]
        slot = (2, 0)[side] + g % 2
        lanes = slice(j * w, (j + 1) * w)
        return remote(
            c3.at[:, :, lanes], kv3.at[:, slot, pl.ds(pl.multiple_of(p * r3, r3), r3)],
            s_l3.at[side, u, j], r_l3.at[slot, p], (2 * (c + dc) + u) * G + j,
        )

    def l3_recv(side, u, j):
        slot = 2 * side + u
        dc = (-1, 1)[side]
        lanes = slice(j * w, (j + 1) * w)
        return remote(
            c3.at[:, :, lanes], kv3.at[:, slot, pl.ds(j * r3, r3)],
            s_l3.at[side, u, j], r_l3.at[slot, j], (2 * (c + dc) + u) * G + j,
        )

    loads[0].wait()
    loads[1].wait()
    m3_ = mean_matrix(rows, 3)
    for t in range(2):
        c3[t] = dot(m3_, kvm[t]).astype(BF16)
    for side, has in sides3:
        @pl.when(has)
        def _():
            for j in range(G):
                for u in range(2):
                    l3_send(side, u, j).start()

    loads[2].wait()
    i_, t_ = iota2(rows, rows)
    perm = jnp.where(order_of(i_, rows) == t_, 1.0, 0.0).astype(BF16)
    qp[...] = dot(perm, qm[...]).astype(BF16)

    def q_send(hh, i):
        d = flip(p, i, bits)
        return remote(qp.at[:, lanes_of(d, hh)], q0.at[hh, p], s_q.at[hh, i], r_q.at[hh, i], g * G + d)

    def q_recv(hh, i):
        d = flip(p, i, bits)
        return remote(qp.at[:, lanes_of(d, hh)], q0.at[hh, d], s_q.at[hh, i], r_q.at[hh, i], g * G + d)

    for hh in heads:
        for i in others:
            q_send(hh, i).start()
    for hh in heads:
        q0[hh, p] = qp[:, lanes_of(p, hh)]

    for has, b0, b1, b2 in ((has_lo, 0, 0, 0), (has_hi, G + 1, 3, 1)):
        @pl.when(jnp.logical_not(has))
        def _():
            kv0[:, :, b0] = jnp.zeros((hg, 2, rows, D), BF16)
            kv1[:, :, b1] = jnp.zeros((hg, 2, LEAF, D), BF16)
            kv2[:, :, b2] = jnp.zeros((hg, 2, LEAF, D), BF16)
    for side, has in sides3:
        @pl.when(jnp.logical_not(has))
        def _():
            kv3[:, 2 * side : 2 * side + 2] = jnp.zeros((2, 2, LEAF // 2, w), BF16)

    def z_pair(hh, dirn, kind):
        last = dirn == 0
        if kind == 0:
            src, dst = (
                (kv0.at[hh, :, G], kv0.at[hh, :, 0]) if last else (kv0.at[hh, :, 1], kv0.at[hh, :, G + 1])
            )
        elif kind == 1:
            a, b = (0, LEAF - r2) if last else (r2, LEAF - r2)
            src, dst = kv2own.at[hh, :, pl.ds(a, b)], kv2.at[hh, :, 0 if last else 1, pl.ds(a, b)]
        else:
            a, b = (0, LEAF - r1) if last else (r1, LEAF - r1)
            src = kv1.at[hh, :, 2 if last else 1, pl.ds(a, b)]
            dst = kv1.at[hh, :, 0 if last else 3, pl.ds(a, b)]
        to = s + G if last else s - G
        return remote(src, dst, s_z.at[hh, dirn, kind], r_z.at[hh, dirn, kind], to)

    dirs = ((0, has_hi), (1, has_lo))
    comes = ((0, has_lo), (1, has_hi))

    def z_start(hh, kind):
        for dirn, has in dirs:
            @pl.when(has)
            def _():
                z_pair(hh, dirn, kind).start()

    def z_wait(hh, kind):
        for dirn, has in comes:
            @pl.when(has)
            def _():
                z_pair(hh, dirn, kind).wait_recv()

    m1_ = mean_matrix(rows, 1)
    m2_ = mean_matrix(rows, 2)
    for copy in own:
        copy.wait()
    for hh in heads:
        for t in range(2):
            for i in others:
                kv_recv(hh, t, i).wait_recv()
        z_start(hh, 0)
        for t in range(2):
            for j in range(G):
                kv2own[hh, t, j * r2 : (j + 1) * r2] = dot(m2_, kv0[hh, t, 1 + j]).astype(BF16)
        z_start(hh, 1)
        for t in range(2):
            for j in range(G):
                at = (j % 2) * r1
                kv1[hh, t, 1 + j // 2, at : at + r1] = dot(m1_, kv0[hh, t, 1 + j]).astype(BF16)
        z_start(hh, 2)

    def bias_of(keys, lo, hi):
        col = lax.broadcasted_iota(jnp.int32, (1, keys), 1)
        b_lo = jnp.where(lo, 0.0, LOWEST)
        b_hi = jnp.where(hi, 0.0, LOWEST)
        return jnp.where(col < LEAF, b_lo, jnp.where(col >= keys - LEAF, b_hi, 0.0))

    def wide(x):
        return jnp.broadcast_to(x, (x.shape[0], D))

    for side, has in sides3:
        @pl.when(has)
        def _():
            for u in range(2):
                for j in range(G):
                    l3_recv(side, u, j).wait_recv()

    state = []
    for hh in heads:
        for i in others:
            q_recv(hh, i).wait_recv()
        for j in range(G):
            x = q0[hh, j].astype(F32)
            x = x[:r1] + x[r1:]
            q1[hh, j] = (x * 0.5).astype(BF16)
            x = x[:r2] + x[r2:]
            q2[hh, j] = (x * 0.25).astype(BF16)
            x = x[:r3] + x[r3:]
            q3[hh, j] = (x * 0.125).astype(BF16)
        lanes = slice(hh * D, (hh + 1) * D)
        top, num = attend(
            q3[hh].reshape(G * r3, D),
            kv3[0, :, :, lanes].reshape(2 * LEAF, D),
            kv3[1, :, :, lanes].reshape(2 * LEAF, D),
            bias_of(2 * LEAF, has_lo3, has_hi3), None,
        )
        state.append((twice(wide(top), G), twice(num, G)))

    for hh in heads:
        z_wait(hh, 0)
    for has, b0, b1, a1, b2, a2 in (
        (has_lo, 0, 0, LEAF - r1, 0, LEAF - r2), (has_hi, G + 1, 3, 0, 1, 0)
    ):
        @pl.when(has)
        def _():
            for hh in heads:
                for t in range(2):
                    x = kv0[hh, t, b0]
                    kv1[hh, t, b1, a1 : a1 + r1] = dot(m1_, x).astype(BF16)
                    kv2[hh, t, b2, a2 : a2 + r2] = dot(m2_, x).astype(BF16)
    for hh in heads:
        z_wait(hh, 1)
        top, num = attend(
            q2[hh].reshape(G * r2, D),
            kv2[hh, 0].reshape(2 * LEAF, D), kv2[hh, 1].reshape(2 * LEAF, D),
            bias_of(2 * LEAF, has_lo, has_hi), state[hh],
        )
        state[hh] = (twice(wide(top), G), twice(num, G))
    for hh in heads:
        z_wait(hh, 2)
        for b in range(2):
            part = slice(b * LEAF, (b + 1) * LEAF)
            top, num = attend(
                q1[hh, 2 * b : 2 * b + 2].reshape(LEAF, D),
                jnp.concatenate([kv1[hh, 0, b], kv1[hh, 0, b + 2]], 0),
                jnp.concatenate([kv1[hh, 1, b], kv1[hh, 1, b + 2]], 0),
                bias_of(2 * LEAF, has_lo if b == 0 else True, has_hi if b == 1 else True),
                (state[hh][0][part], state[hh][1][part]),
            )
            m1[hh, 2 * b : 2 * b + 2] = wide(top).reshape(2, r1, D)
            n1[hh, 2 * b : 2 * b + 2] = num.reshape(2, r1, 2 * D)

    def a_send(i):
        d = flip(p, i, bits)
        return remote(attbuf.at[d], arecv.at[p], s_a.at[i], r_a.at[i], g * G + d)

    def a_recv(i):
        d = flip(p, i, bits)
        return remote(attbuf.at[d], arecv.at[d], s_a.at[i], r_a.at[i], g * G + d)

    def level0(step, carry):
        i = G - 1 - step
        j = flip(p, i, bits)
        bias = bias_of(3 * LEAF, jnp.logical_or(has_lo, j > 0), jnp.logical_or(has_hi, j < G - 1))
        for hh in heads:
            top, num = attend(
                q0[hh, j],
                kv0[hh, 0, pl.ds(j, 3)].reshape(3 * LEAF, D),
                kv0[hh, 1, pl.ds(j, 3)].reshape(3 * LEAF, D),
                bias, (twice(m1[hh, j], 1), twice(n1[hh, j], 1)),
            )
            attbuf[j, :, hh * D : (hh + 1) * D] = (num[:, :D] / num[:, D:]).astype(BF16)

        @pl.when(step < G - 1)
        def _():
            a_send(i).start()

        return carry

    lax.fori_loop(0, G, level0, 0)

    back = jnp.where(order_of(t_, rows) == i_, 1.0, 0.0).astype(BF16)

    def place(d, x):
        att[:, pl.ds(pl.multiple_of(d * w, D), w)] = dot(back, x).astype(BF16)

    place(p, attbuf[p])
    for i in others:
        a_recv(i).wait_recv()
        d = flip(p, i, bits)
        place(d, arecv[d])

    copy_w.wait()
    cw = o_ref.shape[1]
    chunks = psend.shape[1]
    ch = cw // chunks

    def p_copy(i, n, peer):
        return remote(psend.at[i - 1, n], precv.at[i - 1, n], s_p.at[i - 1, n], r_p.at[i - 1, n], None, peer)

    for i in range(1, NH):
        t = (h + i) % NH
        for n in range(chunks):
            at = pl.multiple_of(t * cw + n * ch, D)
            psend[i - 1, n] = dot(att[...], wv[:, pl.ds(at, ch)]).astype(BF16)
            p_copy(i, n, t).start()
    for n in range(chunks):
        at = pl.multiple_of(h * cw + n * ch, D)
        total = dot(att[...], wv[:, pl.ds(at, ch)]).astype(BF16).astype(F32)
        for i in range(1, NH):
            p_copy(i, n, (h + NH - i) % NH).wait_recv()
            total = total + precv[i - 1, n].astype(F32)
        o_ref[:, n * ch : (n + 1) * ch] = total.astype(o_ref.dtype)

    for side, has in sides3:
        @pl.when(has)
        def _():
            for j in range(G):
                for u in range(2):
                    l3_send(side, u, j).wait_send()
    for i in others:
        for hh in heads:
            for t in range(2):
                kv_send(hh, t, i).wait_send()
            q_send(hh, i).wait_send()
        a_send(i).wait_send()
    for kind in range(3):
        for hh in heads:
            for dirn, has in dirs:
                @pl.when(has)
                def _():
                    z_pair(hh, dirn, kind).wait_send()
    for i in range(1, NH):
        for n in range(chunks):
            p_copy(i, n, (h + i) % NH).wait_send()


def solution(mesh):
    S, NH = mesh.shape["seq"], mesh.shape["head"]

    def body(queries, key_rows, value_rows, out_weight):
        rows, width = queries.shape
        full = out_weight.shape[1]
        G = GROUP
        D = HEAD_DIM
        w = width // G
        hg = w // D
        assert rows == LEAF and S % (2 * G) == 0 and S >= 4 * G and w % D == 0
        cw = full // NH
        chunks = 2
        dma = pltpu.SemaphoreType.DMA
        V = pltpu.VMEM
        return pl.pallas_call(
            functools.partial(kernel, S, NH),
            out_shape=jax.ShapeDtypeStruct((rows, cw), queries.dtype),
            in_specs=[pl.BlockSpec(memory_space=pl.ANY)] * 4,
            out_specs=pl.BlockSpec(memory_space=pltpu.VMEM),
            scratch_shapes=[
                V((hg, 2, G + 2, rows, D), BF16),
                V((hg, 2, 4, LEAF, D), BF16),
                V((hg, 2, 2, LEAF, D), BF16),
                V((hg, 2, LEAF, D), BF16),
                V((2, 4, LEAF // 2, w), BF16),
                V((2, rows // 8, width), BF16),
                V((2, rows, width), BF16),
                V((rows, width), BF16),
                V((rows, width), BF16),
                V((hg, G, rows, D), BF16),
                V((hg, G, rows // 2, D), BF16),
                V((hg, G, rows // 4, D), BF16),
                V((hg, G, rows // 8, D), BF16),
                V((hg, G, rows // 2, 2 * D), F32),
                V((hg, G, rows // 2, D), F32),
                V((G, rows, w), BF16),
                V((G, rows, w), BF16),
                V((rows, width), BF16),
                V((width, full), BF16),
                V((NH - 1, chunks, rows, cw // chunks), BF16),
                V((NH - 1, chunks, rows, cw // chunks), BF16),
                dma((hg, 2, G)), dma((hg, 2, G)),
                dma((hg, G)), dma((hg, G)),
                dma((2, 2, G)), dma((4, G)),
                dma((hg, 2, 3)), dma((hg, 2, 3)),
                dma((G,)), dma((G,)),
                dma((NH - 1, chunks)), dma((NH - 1, chunks)),
                dma, dma((3,)), dma((hg, 2)),
            ],
            compiler_params=pltpu.CompilerParams(
                collective_id=0, has_side_effects=True, vmem_limit_bytes=VMEM_BYTES
            ),
        )(queries, key_rows, value_rows, out_weight)

    in_specs = (P("seq", "head"), P("seq", "head"), P("seq", "head"), P("head", None))
    return jax.shard_map(body, mesh=mesh, in_specs=in_specs, out_specs=P("seq", "head"), check_vma=False)
```

```python
import functools
import math

import jax
import jax.numpy as jnp
from jax import lax
from jax.experimental import pallas as pl
from jax.experimental.pallas import tpu as pltpu
from jax.sharding import PartitionSpec as P

HEAD_DIM = 128
LEAF = 256
LEVELS = 3
GROUP = 2 ** (LEVELS - 1)
MESH = pl.DeviceIdType.MESH
SCALE = HEAD_DIM ** (-0.5) * math.log2(math.e)
LOWEST = -1e30
F32 = jnp.float32
BF16 = jnp.bfloat16
VMEM_BYTES = 24 * 2**20


def dot(a, b):
    return lax.dot_general(a, b, (((1,), (0,)), ((), ())), preferred_element_type=F32)


def dot_t(a, b):
    return lax.dot_general(a, b, (((1,), (1,)), ((), ())), preferred_element_type=F32)


def iota2(n, m):
    shape = (n, m)
    return lax.broadcasted_iota(jnp.int32, shape, 0), lax.broadcasted_iota(jnp.int32, shape, 1)


def mean_matrix(rows, level):
    r, c = iota2(rows >> level, rows)
    return jnp.where((c >> level) == r, 0.5**level, 0.0).astype(BF16)


def order_of(i, rows):
    top = rows.bit_length() - 1
    row = (i & (rows // 2**LEVELS - 1)) << LEVELS
    for bit in range(LEVELS):
        row = row | (((i >> (top - 1 - bit)) & 1) << bit)
    return row


def flip(p, i, bits):
    out = 0
    for b in range(bits):
        out = out + 2**b * ((p // 2**b + i // 2**b) % 2)
    return out


def attend(q, k, v, bias, before):
    s = dot_t(q, k)
    if bias is not None:
        s = s + bias
    top = jnp.max(s, axis=1, keepdims=True) * SCALE
    if before is not None:
        coarse_top, coarse_num = before
        top = jnp.maximum(top, coarse_top[:, :1])
    w = jnp.exp2(s * SCALE - top).astype(BF16)
    num = dot(w, jnp.concatenate([v, jnp.ones((v.shape[0], HEAD_DIM), BF16)], 1))
    if before is not None:
        a = 2.0 * jnp.exp2(coarse_top - top)
        num = num + jnp.concatenate([a, a], 1) * coarse_num
    return top, num


def twice(x, pieces):
    n = x.shape[0] // pieces
    out = []
    for i in range(pieces):
        out += [x[i * n : (i + 1) * n], x[i * n : (i + 1) * n]]
    return jnp.concatenate(out, 0)


def kernel(
    S, NH, q_hbm, k_hbm, v_hbm, w_hbm, o_ref,
    kv0, kv1, kv2, kv2own, kv3, c3, kvm, qm, qp, q0, q1, q2, q3, n1, m1,
    attbuf, arecv, att, acc, wv, psend, precv,
    s_kv, r_kv, s_q, r_q, s_l3, r_l3, s_z, r_z, s_a, r_a, s_p, r_p, s_w, s_in, s_own,
):
    rows, width = q_hbm.shape
    G = GROUP
    D = HEAD_DIM
    w = width // G
    hg = w // D
    NG = S // G
    bits = G.bit_length() - 1
    s = lax.axis_index("seq")
    h = lax.axis_index("head")
    g = s // G
    p = s % G
    c = g // 2
    blocks3 = NG // 2
    has_lo, has_hi = g > 0, g < NG - 1
    has_lo3, has_hi3 = c > 0, c < blocks3 - 1
    sides3 = ((0, has_lo3), (1, has_hi3))
    r1, r2, r3 = rows // 2, rows // 4, rows // 8
    heads = range(hg)
    others = tuple(range(G - 1, 0, -1))

    barrier = pltpu.get_barrier_semaphore()
    for i in others:
        pl.semaphore_signal(barrier, 1, device_id={"seq": g * G + flip(p, i, bits)}, device_id_type=MESH)
    for i in range(1, NH):
        pl.semaphore_signal(barrier, 1, device_id={"head": (h + i) % NH}, device_id_type=MESH)
    sibling = g + 1 - 2 * (g % 2)
    pl.semaphore_signal(barrier, 1, device_id={"seq": sibling * G + p}, device_id_type=MESH)
    for has, dc in ((has_lo3, -1), (has_hi3, 1)):
        @pl.when(has)
        def _():
            for u in range(2):
                for j in range(G):
                    pl.semaphore_signal(
                        barrier, 1, device_id={"seq": (2 * (c + dc) + u) * G + j}, device_id_type=MESH
                    )

    kv_hbm = (k_hbm, v_hbm)
    loads = [pltpu.make_async_copy(kv_hbm[t], kvm.at[t], s_in.at[t]) for t in range(2)]
    loads.append(pltpu.make_async_copy(q_hbm, qm, s_in.at[2]))
    for load in (loads[2], loads[0], loads[1]):
        load.start()
    copy_w = pltpu.make_async_copy(w_hbm, wv, s_w)

    def lanes_of(i, hh):
        return pl.ds(pl.multiple_of((i * hg + hh) * D, D), D)

    def remote(src, dst, ss, rs, seq, head=None):
        ids = {"seq": seq} if head is None else {"head": head}
        return pltpu.make_async_remote_copy(
            src_ref=src, dst_ref=dst, send_sem=ss, recv_sem=rs, device_id=ids, device_id_type=MESH
        )

    own = []
    for hh in heads:
        for t in range(2):
            own.append(
                pltpu.make_async_copy(kv_hbm[t].at[:, lanes_of(p, hh)], kv0.at[hh, t, 1 + p], s_own.at[hh, t])
            )
            own[-1].start()

    sides = jnp.where(has_lo3, 1, 0) + jnp.where(has_hi3, 1, 0)
    pl.semaphore_wait(barrier, G - 1 + NH - 1 + 1 + 2 * G * sides)

    def kv_send(hh, t, i):
        d = flip(p, i, bits)
        return remote(
            kv_hbm[t].at[:, lanes_of(d, hh)], kv0.at[hh, t, 1 + p], s_kv.at[hh, t, i], r_kv.at[hh, t, i], g * G + d
        )

    def kv_recv(hh, t, i):
        d = flip(p, i, bits)
        return remote(
            kv_hbm[t].at[:, lanes_of(d, hh)], kv0.at[hh, t, 1 + d], s_kv.at[hh, t, i], r_kv.at[hh, t, i], g * G + d
        )

    for hh in heads:
        for t in range(2):
            for i in others:
                kv_send(hh, t, i).start()
    copy_w.start()

    def l3_send(side, u, j):
        dc = (-1, 1)[side]
        slot = (2, 0)[side] + g % 2
        lanes = slice(j * w, (j + 1) * w)
        return remote(
            c3.at[:, :, lanes], kv3.at[:, slot, pl.ds(pl.multiple_of(p * r3, r3), r3)],
            s_l3.at[side, u, j], r_l3.at[slot, p], (2 * (c + dc) + u) * G + j,
        )

    def l3_recv(side, u, j):
        slot = 2 * side + u
        dc = (-1, 1)[side]
        lanes = slice(j * w, (j + 1) * w)
        return remote(
            c3.at[:, :, lanes], kv3.at[:, slot, pl.ds(j * r3, r3)],
            s_l3.at[side, u, j], r_l3.at[slot, j], (2 * (c + dc) + u) * G + j,
        )

    loads[0].wait()
    loads[1].wait()
    m3_ = mean_matrix(rows, 3)
    for t in range(2):
        c3[t] = dot(m3_, kvm[t]).astype(BF16)
    for side, has in sides3:
        @pl.when(has)
        def _():
            for j in range(G):
                for u in range(2):
                    l3_send(side, u, j).start()

    loads[2].wait()
    i_, t_ = iota2(rows, rows)
    perm = jnp.where(order_of(i_, rows) == t_, 1.0, 0.0).astype(BF16)
    qp[...] = dot(perm, qm[...]).astype(BF16)

    def q_send(hh, i):
        d = flip(p, i, bits)
        return remote(qp.at[:, lanes_of(d, hh)], q0.at[hh, p], s_q.at[hh, i], r_q.at[hh, i], g * G + d)

    def q_recv(hh, i):
        d = flip(p, i, bits)
        return remote(qp.at[:, lanes_of(d, hh)], q0.at[hh, d], s_q.at[hh, i], r_q.at[hh, i], g * G + d)

    for hh in heads:
        for i in others:
            q_send(hh, i).start()
    for hh in heads:
        q0[hh, p] = qp[:, lanes_of(p, hh)]

    for has, b0, b1, b2 in ((has_lo, 0, 0, 0), (has_hi, G + 1, 3, 1)):
        @pl.when(jnp.logical_not(has))
        def _():
            kv0[:, :, b0] = jnp.zeros((hg, 2, rows, D), BF16)
            kv1[:, :, b1] = jnp.zeros((hg, 2, LEAF, D), BF16)
            kv2[:, :, b2] = jnp.zeros((hg, 2, LEAF, D), BF16)
    for side, has in sides3:
        @pl.when(jnp.logical_not(has))
        def _():
            kv3[:, 2 * side : 2 * side + 2] = jnp.zeros((2, 2, LEAF // 2, w), BF16)

    def z_pair(hh, dirn, kind):
        last = dirn == 0
        if kind == 0:
            src, dst = (
                (kv0.at[hh, :, G], kv0.at[hh, :, 0]) if last else (kv0.at[hh, :, 1], kv0.at[hh, :, G + 1])
            )
        elif kind == 1:
            a, b = (0, LEAF - r2) if last else (r2, LEAF - r2)
            src, dst = kv2own.at[hh, :, pl.ds(a, b)], kv2.at[hh, :, 0 if last else 1, pl.ds(a, b)]
        else:
            a, b = (0, LEAF - r1) if last else (r1, LEAF - r1)
            src = kv1.at[hh, :, 2 if last else 1, pl.ds(a, b)]
            dst = kv1.at[hh, :, 0 if last else 3, pl.ds(a, b)]
        to = s + G if last else s - G
        return remote(src, dst, s_z.at[hh, dirn, kind], r_z.at[hh, dirn, kind], to)

    dirs = ((0, has_hi), (1, has_lo))
    comes = ((0, has_lo), (1, has_hi))

    def z_start(hh, kind):
        for dirn, has in dirs:
            @pl.when(has)
            def _():
                z_pair(hh, dirn, kind).start()

    def z_wait(hh, kind):
        for dirn, has in comes:
            @pl.when(has)
            def _():
                z_pair(hh, dirn, kind).wait_recv()

    m1_ = mean_matrix(rows, 1)
    m2_ = mean_matrix(rows, 2)
    for copy in own:
        copy.wait()
    for hh in heads:
        for t in range(2):
            for i in others:
                kv_recv(hh, t, i).wait_recv()
        z_start(hh, 0)
        for t in range(2):
            for j in range(G):
                kv2own[hh, t, j * r2 : (j + 1) * r2] = dot(m2_, kv0[hh, t, 1 + j]).astype(BF16)
        z_start(hh, 1)
        for t in range(2):
            for j in range(G):
                at = (j % 2) * r1
                kv1[hh, t, 1 + j // 2, at : at + r1] = dot(m1_, kv0[hh, t, 1 + j]).astype(BF16)
        z_start(hh, 2)

    def bias_of(keys, lo, hi):
        col = lax.broadcasted_iota(jnp.int32, (1, keys), 1)
        b_lo = jnp.where(lo, 0.0, LOWEST)
        b_hi = jnp.where(hi, 0.0, LOWEST)
        return jnp.where(col < LEAF, b_lo, jnp.where(col >= keys - LEAF, b_hi, 0.0))

    def wide(x):
        return jnp.broadcast_to(x, (x.shape[0], D))

    for side, has in sides3:
        @pl.when(has)
        def _():
            for u in range(2):
                for j in range(G):
                    l3_recv(side, u, j).wait_recv()

    edges = ((has_lo, 0, 0, LEAF - r1, 0, LEAF - r2), (has_hi, G + 1, 3, 0, 1, 0))

    def a_send(hh, i):
        d = flip(p, i, bits)
        return remote(attbuf.at[hh, d], arecv.at[hh, p], s_a.at[hh, i], r_a.at[hh, i], g * G + d)

    def a_recv(hh, i):
        d = flip(p, i, bits)
        return remote(attbuf.at[hh, d], arecv.at[hh, d], s_a.at[hh, i], r_a.at[hh, i], g * G + d)

    for hh in heads:
        for i in others:
            q_recv(hh, i).wait_recv()
        for j in range(G):
            x = q0[hh, j].astype(F32)
            x = x[:r1] + x[r1:]
            q1[hh, j] = (x * 0.5).astype(BF16)
            x = x[:r2] + x[r2:]
            q2[hh, j] = (x * 0.25).astype(BF16)
            x = x[:r3] + x[r3:]
            q3[hh, j] = (x * 0.125).astype(BF16)
        lanes = slice(hh * D, (hh + 1) * D)
        top, num = attend(
            q3[hh].reshape(G * r3, D),
            kv3[0, :, :, lanes].reshape(2 * LEAF, D),
            kv3[1, :, :, lanes].reshape(2 * LEAF, D),
            bias_of(2 * LEAF, has_lo3, has_hi3), None,
        )
        state = (twice(wide(top), G), twice(num, G))
        z_wait(hh, 0)
        for has, b0, b1, a1, b2, a2 in edges:
            @pl.when(has)
            def _():
                for t in range(2):
                    x = kv0[hh, t, b0]
                    kv1[hh, t, b1, a1 : a1 + r1] = dot(m1_, x).astype(BF16)
                    kv2[hh, t, b2, a2 : a2 + r2] = dot(m2_, x).astype(BF16)
        z_wait(hh, 1)
        top, num = attend(
            q2[hh].reshape(G * r2, D),
            kv2[hh, 0].reshape(2 * LEAF, D), kv2[hh, 1].reshape(2 * LEAF, D),
            bias_of(2 * LEAF, has_lo, has_hi), state,
        )
        state = (twice(wide(top), G), twice(num, G))
        z_wait(hh, 2)
        for b in range(2):
            part = slice(b * LEAF, (b + 1) * LEAF)
            top, num = attend(
                q1[hh, 2 * b : 2 * b + 2].reshape(LEAF, D),
                jnp.concatenate([kv1[hh, 0, b], kv1[hh, 0, b + 2]], 0),
                jnp.concatenate([kv1[hh, 1, b], kv1[hh, 1, b + 2]], 0),
                bias_of(2 * LEAF, has_lo if b == 0 else True, has_hi if b == 1 else True),
                (state[0][part], state[1][part]),
            )
            m1[hh, 2 * b : 2 * b + 2] = wide(top).reshape(2, r1, D)
            n1[hh, 2 * b : 2 * b + 2] = num.reshape(2, r1, 2 * D)
        for i in others + (0,):
            j = flip(p, i, bits)
            bias = bias_of(3 * LEAF, jnp.logical_or(has_lo, j > 0), jnp.logical_or(has_hi, j < G - 1))
            top, num = attend(
                q0[hh, j],
                kv0[hh, 0, pl.ds(j, 3)].reshape(3 * LEAF, D),
                kv0[hh, 1, pl.ds(j, 3)].reshape(3 * LEAF, D),
                bias, (twice(m1[hh, j], 1), twice(n1[hh, j], 1)),
            )
            attbuf[hh, j] = (num[:, :D] / num[:, D:]).astype(BF16)
            if i:
                a_send(hh, i).start()

    back = jnp.where(order_of(t_, rows) == i_, 1.0, 0.0).astype(BF16)
    cw = o_ref.shape[1]
    chunks = psend.shape[1]
    ch = cw // chunks
    copy_w.wait()

    def project(hh, at):
        lanes = pl.ds(at if isinstance(at, int) else pl.multiple_of(at, D), ch)
        weight = jnp.concatenate([wv[(d * hg + hh) * D : (d * hg + hh + 1) * D, lanes] for d in range(G)], 0)
        out = dot(att[hh], weight)
        return out if hh == 0 else out + acc[:, lanes]

    def p_copy(i, n, peer):
        return remote(psend.at[i - 1, n], precv.at[i - 1, n], s_p.at[i - 1, n], r_p.at[i - 1, n], None, peer)

    for hh in heads:
        arecv[hh, p] = attbuf[hh, p]
        for i in others:
            a_recv(hh, i).wait_recv()
        for d in range(G):
            att[hh, :, d * D : (d + 1) * D] = dot(back, arecv[hh, d]).astype(BF16)
        if hh < hg - 1:
            for n in range(NH * chunks):
                acc[:, n * ch : (n + 1) * ch] = project(hh, n * ch)
    last = hg - 1
    for i in range(1, NH):
        t = (h + i) % NH
        for n in range(chunks):
            psend[i - 1, n] = project(last, t * cw + n * ch).astype(BF16)
            p_copy(i, n, t).start()
    for n in range(chunks):
        total = project(last, h * cw + n * ch).astype(BF16).astype(F32)
        for i in range(1, NH):
            p_copy(i, n, (h + NH - i) % NH).wait_recv()
            total = total + precv[i - 1, n].astype(F32)
        o_ref[:, n * ch : (n + 1) * ch] = total.astype(o_ref.dtype)

    for side, has in sides3:
        @pl.when(has)
        def _():
            for j in range(G):
                for u in range(2):
                    l3_send(side, u, j).wait_send()
    for i in others:
        for hh in heads:
            for t in range(2):
                kv_send(hh, t, i).wait_send()
            q_send(hh, i).wait_send()
            a_send(hh, i).wait_send()
    for kind in range(3):
        for hh in heads:
            for dirn, has in dirs:
                @pl.when(has)
                def _():
                    z_pair(hh, dirn, kind).wait_send()
    for i in range(1, NH):
        for n in range(chunks):
            p_copy(i, n, (h + i) % NH).wait_send()


def solution(mesh):
    S, NH = mesh.shape["seq"], mesh.shape["head"]

    def body(queries, key_rows, value_rows, out_weight):
        rows, width = queries.shape
        full = out_weight.shape[1]
        G = GROUP
        D = HEAD_DIM
        w = width // G
        hg = w // D
        assert rows == LEAF and S % (2 * G) == 0 and S >= 4 * G and w % D == 0
        cw = full // NH
        chunks = 2
        dma = pltpu.SemaphoreType.DMA
        V = pltpu.VMEM
        return pl.pallas_call(
            functools.partial(kernel, S, NH),
            out_shape=jax.ShapeDtypeStruct((rows, cw), queries.dtype),
            in_specs=[pl.BlockSpec(memory_space=pltpu.HBM)] * 4,
            out_specs=pl.BlockSpec(memory_space=pltpu.VMEM),
            scratch_shapes=[
                V((hg, 2, G + 2, rows, D), BF16),
                V((hg, 2, 4, LEAF, D), BF16),
                V((hg, 2, 2, LEAF, D), BF16),
                V((hg, 2, LEAF, D), BF16),
                V((2, 4, LEAF // 2, w), BF16),
                V((2, rows // 8, width), BF16),
                V((2, rows, width), BF16),
                V((rows, width), BF16),
                V((rows, width), BF16),
                V((hg, G, rows, D), BF16),
                V((hg, G, rows // 2, D), BF16),
                V((hg, G, rows // 4, D), BF16),
                V((hg, G, rows // 8, D), BF16),
                V((hg, G, rows // 2, 2 * D), F32),
                V((hg, G, rows // 2, D), F32),
                V((hg, G, rows, D), BF16),
                V((hg, G, rows, D), BF16),
                V((hg, rows, G * D), BF16),
                V((rows, full), F32),
                V((width, full), BF16),
                V((NH - 1, chunks, rows, cw // chunks), BF16),
                V((NH - 1, chunks, rows, cw // chunks), BF16),
                dma((hg, 2, G)), dma((hg, 2, G)),
                dma((hg, G)), dma((hg, G)),
                dma((2, 2, G)), dma((4, G)),
                dma((hg, 2, 3)), dma((hg, 2, 3)),
                dma((hg, G)), dma((hg, G)),
                dma((NH - 1, chunks)), dma((NH - 1, chunks)),
                dma, dma((3,)), dma((hg, 2)),
            ],
            compiler_params=pltpu.CompilerParams(
                collective_id=0, has_side_effects=True, vmem_limit_bytes=VMEM_BYTES
            ),
        )(*[pltpu.with_memory_space_constraint(x, pltpu.HBM) for x in (queries, key_rows, value_rows, out_weight)])

    in_specs = (P("seq", "head"), P("seq", "head"), P("seq", "head"), P("head", None))
    return jax.shard_map(body, mesh=mesh, in_specs=in_specs, out_specs=P("seq", "head"), check_vma=False)
```
